768 devices in a mesh: ctx: 32 (over x, y_hi, core), section: 24 (over y_lo, z).
Axes of the slice: x: 4, y: 8 (y_hi: 4, y_lo: 2; y = y_hi * 2 + y_lo), z: 12, core: 2. Of those that a mesh axis runs over, the one named last changes fastest.
Arguments:
- queries: bfloat16 [24, 4096, 4096], P('section', 'ctx'), may hold values from -24 to 24
- keys: bfloat16 [24, 4096, 512], P('section', 'ctx'), may hold values from -24 to 24
- values: bfloat16 [24, 4096, 512], P('section', 'ctx'), may hold values from -6 to 6
- doc_lengths: int32 [24, 4], P('section'), may hold values from 1 to 2048, 4096 in all within a row
- interp_num: int32 [1], replicated, may hold values from 250 to 999
- interp_den: int32 [1], replicated, may hold values from 1000 to 1999
Outputs:
- handed: bfloat16 [24, 4096, 4096], P('section', 'ctx')
The draws below stay inside these ranges and needn't reach their ends.
Inputs may be any that keep to these rules, and one draw needn't show every extreme that they name: `doc_lengths`: each row sums to 4096; its longest document has exactly 2048 tokens.
All inputs are finite; a program needn't handle non-finite values.
Results may differ from the reference program's by a relative error of at most 0.0099.
Values may be sent and summed in bfloat16 or wider, within the bound.
No kernel may reach another device: no remote copies, remote signals or barrier semaphores. Data moves between devices by JAX's collectives and lax.ppermute only.
A program may use at most 64 MiB of HBM per device.

```python
import math
import jax
import jax.numpy as jnp
import numpy as np
from jax import lax

QUERY_HEADS = 32
KEY_VALUE_HEADS = 4
HEAD_DIMENSION = 128
TOK_DEV = 128
DOCS = 4
SPAN = 64
SEQUENCE_TOKENS = 4096
RELAY_SECTIONS = 24
N_CTX = 32


def random_base_sample(key, heads, salt):
    shape = (RELAY_SECTIONS, SEQUENCE_TOKENS, heads, HEAD_DIMENSION)
    return jnp.clip(jax.random.normal(jax.random.fold_in(key, salt), shape, jnp.float32), -6.0, 6.0)


def draw_queries(key, part):
    input_array = random_base_sample(key, QUERY_HEADS, 11)
    return input_array.reshape(RELAY_SECTIONS, SEQUENCE_TOKENS, QUERY_HEADS * HEAD_DIMENSION).astype(jnp.bfloat16)


def draw_keys(key, part):
    input_array = random_base_sample(key, KEY_VALUE_HEADS, 23)
    return input_array.reshape(RELAY_SECTIONS, SEQUENCE_TOKENS, KEY_VALUE_HEADS * HEAD_DIMENSION).astype(jnp.bfloat16)


def block_levels(key, shape, split, least, largest):
    def one(axis_at, shards_of):
        draws = jax.random.uniform(jax.random.fold_in(jax.random.fold_in(key, 6), axis_at), (shards_of,), jnp.float32, least / len(split), largest / len(split))
        return jnp.repeat(jnp.exp(draws), shape[axis_at] // shards_of).reshape((-1,) + (1,) * (len(shape) - axis_at - 1))

    factor_of = one(*split[0])
    for cut in split[1:]:
        factor_of = factor_of * one(*cut)
    return factor_of


def length_profile(number_of, total, reach, slope):
    weights = [(1 << 20) // math.isqrt(standing ** slope) + 1 for standing in range(2, number_of + 1)]
    spare, given = total - reach - (number_of - 1), [1] * (number_of - 1)
    while spare > 0:
        free = [i for i in range(number_of - 1) if given[i] < reach]
        whole, remaining = sum([weights[i] for i in free]), spare
        for i in free:
            addition = min(reach - given[i], max(1, remaining * weights[i] // whole), spare)
            given[i] = given[i] + addition
            spare = spare - addition
    return np.array([reach] + given)


def uneven_parts(stream_key, count, total, reach, lean):
    if count == 2:
        one = jax.random.randint(stream_key, (), max(1, total - reach), min(reach, total - 1) + 1)
        return jnp.stack([one, total - one])
    sizes = jnp.asarray(length_profile(count, total, reach, lean), jnp.int32)
    twos = (count - 1) // 2
    giver, sink = sizes[1:1 + 2 * twos:2], sizes[2:2 + 2 * twos:2]
    margin = jnp.minimum(giver - 1, reach - sink)
    moved = jax.random.randint(jax.random.fold_in(stream_key, 1), (twos,), 0, 1 << 20) % (margin + 1)
    sizes = sizes.at[1:1 + 2 * twos:2].set(giver - moved).at[2:2 + 2 * twos:2].set(sink + moved)
    return sizes[jax.random.permutation(jax.random.fold_in(stream_key, 2), count)]


def centred(rng, shape, deviation, reach, shards=(), kind=jnp.bfloat16):
    result = jax.random.normal(rng, shape, jnp.float32) * deviation
    if len(shards) > 0:
        result = block_levels(rng, shape, shards, -0.22, 0.18) * result
    return jnp.clip(result, min=-reach, max=reach).astype(kind)


def setup_inputs(seed: int = 0) -> dict:
    splits = jax.random.split(jax.random.key(seed), 7)
    queries = draw_queries(jax.random.fold_in(splits[6], 71), 0)
    keys = draw_keys(jax.random.fold_in(splits[6], 71), 0)
    values = centred(splits[2], (RELAY_SECTIONS, SEQUENCE_TOKENS, KEY_VALUE_HEADS * HEAD_DIMENSION), 1.0, 6.0, ((0, 24), (1, 32)))
    doc_lengths = jax.vmap(lambda own: uneven_parts(own, DOCS, SEQUENCE_TOKENS, SEQUENCE_TOKENS // 2, 2))(jax.random.split(splits[3], RELAY_SECTIONS)).reshape((RELAY_SECTIONS, DOCS)).astype(jnp.int32)
    interp_num = jax.random.randint(splits[4], (1,), 250, 1000).astype(jnp.int32)
    interp_den = jax.random.randint(splits[5], (1,), 1000, 2000).astype(jnp.int32)
    return {"queries": queries, "keys": keys, "values": values, "doc_lengths": doc_lengths, "interp_num": interp_num, "interp_den": interp_den}


THETA = 500000.0
document_masked_scores = -1e+30

def document_info(positions, lengths):
    doc_ends = jnp.cumsum(lengths).astype(jnp.int32)
    passed = positions[:, None] >= doc_ends[None, :]
    doc_ids = lax.optimization_barrier(jnp.sum(passed.astype(jnp.int32), axis=1)).astype(jnp.int32)
    starts = lax.optimization_barrier(jnp.sum(jnp.where(passed, lengths[None, :], 0), axis=1)).astype(jnp.int32)
    return (doc_ids, (positions - starts).astype(jnp.int32))

def rotation_tables(input_array, position_starts, stretch_factor):
    half_size = HEAD_DIMENSION // 2
    inverse_freq = THETA ** (-(2.0 * jnp.arange(half_size, dtype=jnp.float32)) / HEAD_DIMENSION)
    angles = position_starts.astype(jnp.float32)[:, None] * stretch_factor * inverse_freq[None, :]
    cosine = jnp.cos(angles)[:, None, :]
    sine = jnp.sin(angles)[:, None, :]
    widened = input_array.astype(jnp.float32)
    first_half = widened[..., :half_size]
    second_half = widened[..., half_size:]
    joined = jnp.concatenate([first_half * cosine - second_half * sine, second_half * cosine + first_half * sine], axis=-1)
    return joined.astype(jnp.bfloat16)

def fold_positions(rows):
    shard = rows // TOK_DEV
    within = rows % TOK_DEV
    return jnp.where(within < SPAN, shard * SPAN + within, (2 * N_CTX - 1 - shard) * SPAN + within - SPAN).astype(jnp.int32)

def unfold_rows(positions):
    block_number = positions // SPAN
    within = positions % SPAN
    return jnp.where(block_number < N_CTX, block_number * TOK_DEV + within, (2 * N_CTX - 1 - block_number) * TOK_DEV + SPAN + within).astype(jnp.int32)

def reference(queries, keys, values, doc_lengths, interp_num, interp_den):
    stretch_factor = interp_num[0].astype(jnp.float32) / interp_den[0].astype(jnp.float32)
    query_group_width = QUERY_HEADS // KEY_VALUE_HEADS
    score_scale = 1.0 / math.sqrt(HEAD_DIMENSION)
    sequence = jnp.arange(SEQUENCE_TOKENS, dtype=jnp.int32)
    sequence_row_count = unfold_rows(sequence)
    folded_pos = fold_positions(sequence)
    block_rows = min(512, SEQUENCE_TOKENS)

    def one_section(inputs):
        queries_per_section, keys_per_section, values_per_section, lengths = inputs
        doc_ids, position_starts = document_info(sequence, lengths)
        turned_queries = rotation_tables(queries_per_section[sequence_row_count].reshape(SEQUENCE_TOKENS, QUERY_HEADS, HEAD_DIMENSION), position_starts, stretch_factor).reshape(SEQUENCE_TOKENS, KEY_VALUE_HEADS, query_group_width, HEAD_DIMENSION)
        turned_keys = rotation_tables(keys_per_section[sequence_row_count].reshape(SEQUENCE_TOKENS, KEY_VALUE_HEADS, HEAD_DIMENSION), position_starts, stretch_factor)
        sorted_value_rows = values_per_section[sequence_row_count].reshape(SEQUENCE_TOKENS, KEY_VALUE_HEADS, HEAD_DIMENSION)
        outputs = []
        for block_number in range(SEQUENCE_TOKENS // block_rows):
            low_row = block_number * block_rows
            high_row = low_row + block_rows
            query_block = turned_queries[low_row:high_row].astype(jnp.float32)
            current_key_block = turned_keys[:high_row].astype(jnp.float32)
            scores = jnp.einsum('qhgd,khd->qhgk', query_block, current_key_block) * score_scale
            allowed = (sequence[:high_row][None, :] <= sequence[low_row:high_row][:, None]) & (doc_ids[:high_row][None, :] == doc_ids[low_row:high_row][:, None])
            scores = jnp.where(allowed[:, None, None, :], scores, document_masked_scores)
            weights = jax.nn.softmax(scores, axis=-1).astype(jnp.bfloat16)
            attended = jnp.einsum('qhgk,khd->qhgd', weights.astype(jnp.float32), sorted_value_rows[:high_row].astype(jnp.float32))
            outputs.append(attended.astype(jnp.bfloat16).reshape(block_rows, QUERY_HEADS * HEAD_DIMENSION))
        in_order = jnp.concatenate(outputs, axis=0)
        return in_order[folded_pos]
    attended_all = lax.map(one_section, (queries, keys, values, doc_lengths))
    return jnp.roll(attended_all, 1, axis=0)
```

```python
import functools
import math

import jax
import jax.numpy as jnp
import numpy as np
from jax import lax
from jax.experimental import pallas as pl
from jax.experimental.pallas import tpu as pltpu
from jax.sharding import Mesh, PartitionSpec as P

KV_HEADS = 4
GROUP = 8
HEAD = 128
THETA = 500000.0
MASKED = -1e30
SPAN = 64
TILE = 256
PER_TILE = TILE // SPAN
QUERY_SCALE = math.log2(math.e) / math.sqrt(HEAD)
AXES = ("x", "yh", "c", "yl", "z")
SIZES = (4, 4, 2, 2, 12)


def route(dx, ds):
    pairs = []
    for i in range(math.prod(SIZES)):
        x, yh, c, yl, z = (int(a) for a in np.unravel_index(i, SIZES))
        s = (yl * SIZES[4] + z + ds) % (SIZES[3] * SIZES[4])
        to = ((x + dx) % 4, yh, c, s // SIZES[4], s % SIZES[4])
        pairs.append((i, int(np.ravel_multi_index(to, SIZES))))
    return pairs


def doc_start(position, lens_ref):
    end = 0
    start = jnp.zeros_like(position)
    for d in range(4):
        length = lens_ref[0, d]
        end = end + length
        start = start + jnp.where(position >= end, length, 0)
    return start


def pack_kernel(where_ref, lens_ref, num_ref, den_ref, freq_ref, q_ref, k_ref, v_ref, qp_ref, kv_ref):
    x = where_ref[0]
    shard = x * 8 + where_ref[1] * 2 + where_ref[2]
    row = lax.broadcasted_iota(jnp.int32, (128, HEAD), 0)
    lane = lax.broadcasted_iota(jnp.int32, (128, HEAD), 1)
    position = jnp.where(row < SPAN, shard * SPAN + row, (63 - shard) * SPAN + row - SPAN)
    offset = (position - doc_start(position, lens_ref)).astype(jnp.float32)
    ratio = jnp.full((128, HEAD), num_ref[0], jnp.int32).astype(jnp.float32) / jnp.full(
        (128, HEAD), den_ref[0], jnp.int32
    ).astype(jnp.float32)
    angle = offset * ratio * freq_ref[...]
    cosine = jnp.cos(angle)
    sine = jnp.sin(angle)
    sine = jnp.where(lane < HEAD // 2, -sine, sine)
    for h in range(KV_HEADS):
        cols = slice(h * HEAD, (h + 1) * HEAD)
        wide = k_ref[:, cols].astype(jnp.float32)
        turned = (wide * cosine + pltpu.roll(wide, HEAD // 2, 1) * sine).astype(jnp.bfloat16)
        value = v_ref[:, cols]
        for y in range(4):
            kv_ref[h * 4 + y, :, :HEAD] = turned
            kv_ref[h * 4 + y, :, HEAD:] = value
    cosine = cosine * QUERY_SCALE
    sine = sine * QUERY_SCALE
    for d in range(4):
        group = lax.rem(x + d, 4)
        for h in range(GROUP):
            start = pl.multiple_of(group * (GROUP * HEAD) + h * HEAD, HEAD)
            wide = q_ref[:, pl.ds(start, HEAD)].astype(jnp.float32)
            turned = wide * cosine + pltpu.roll(wide, HEAD // 2, 1) * sine
            qp_ref[d, :, h * HEAD : (h + 1) * HEAD] = turned.astype(jnp.bfloat16)


def attend_kernel(
    where_ref, lens_ref, q0, q1, q2, q3, own_ref, twin_ref, o0, o1, o2, o3, q_scr, kv_ref, o_scr, s_scr, m_scr, acc_scr
):
    x = where_ref[0]
    base = where_ref[1] * 2 + where_ref[2]
    for d, q in enumerate((q0, q1, q2, q3)):
        q_scr[d] = q[...]
    core = where_ref[2]
    kv_ref[core] = own_ref[...]
    kv_ref[1 - core] = twin_ref[...]
    ones = jnp.ones((TILE, HEAD), jnp.bfloat16)
    row = lax.broadcasted_iota(jnp.int32, (SPAN, TILE), 0)
    lane = lax.broadcasted_iota(jnp.int32, (SPAN, TILE), 1)

    def slot_of(block):
        late = (block >= 32).astype(jnp.int32)
        shard = jnp.where(block >= 32, 63 - block, block)
        return lax.rem(shard, 2), lax.div(shard, 2), late

    def tile_of(t, lo, hi):
        parts = []
        for j in range(PER_TILE):
            core, slot, late = slot_of(t * PER_TILE + j)
            parts.append(kv_ref[core, slot, pl.ds(pl.multiple_of(late * SPAN, SPAN), SPAN), lo:hi])
        return jnp.concatenate(parts, axis=0)

    def one_block(i, _):
        d = lax.div(i, 2)
        half = lax.rem(i, 2)
        rows = pl.ds(pl.multiple_of(half * SPAN, SPAN), SPAN)
        shard = lax.rem(x - d + 4, 4) * 8 + base
        block = jnp.where(half == 0, shard, 63 - shard)
        first = block * SPAN
        t_lo = lax.div(doc_start(first, lens_ref), TILE)
        count = lax.div(first, TILE) - t_lo + 1
        q_tile = jnp.concatenate(
            [q_scr[d, rows, h * HEAD : (h + 1) * HEAD] for h in range(GROUP)], axis=0
        )
        q_pos = first + row
        q_start = doc_start(q_pos, lens_ref)
        m_scr[...] = jnp.full(m_scr.shape, MASKED, jnp.float32)
        acc_scr[...] = jnp.zeros_like(acc_scr)

        def scores(t, _):
            k_tile = tile_of(t_lo + t, 0, HEAD)
            k_pos = (t_lo + t) * TILE + lane
            bias = jnp.where((k_pos <= q_pos) & (k_pos >= q_start), 0.0, MASKED)
            s = lax.dot_general(
                q_tile, k_tile, (((1,), (1,)), ((), ())), preferred_element_type=jnp.float32
            )
            s = (s.reshape(GROUP, SPAN, TILE) + bias[None]).reshape(GROUP * SPAN, TILE)
            s_scr[t] = s
            m_scr[...] = jnp.maximum(m_scr[...], jnp.maximum(s[:, :HEAD], s[:, HEAD:]))
            return 0

        lax.fori_loop(0, count, scores, 0)
        top = jnp.max(m_scr[...], axis=1, keepdims=True)
        m_scr[...] = jnp.broadcast_to(top, m_scr.shape)

        def weigh(t, _):
            m = m_scr[...]
            w = jnp.exp2(s_scr[t] - jnp.concatenate([m, m], axis=1)).astype(jnp.bfloat16)
            v_tile = jnp.concatenate([tile_of(t_lo + t, HEAD, 2 * HEAD), ones], axis=1)
            acc_scr[...] += jnp.dot(w, v_tile, preferred_element_type=jnp.float32)
            return 0

        lax.fori_loop(0, count, weigh, 0)
        out = (acc_scr[:, :HEAD] / acc_scr[:, HEAD:]).astype(jnp.bfloat16)
        for h in range(GROUP):
            o_scr[d, rows, h * HEAD : (h + 1) * HEAD] = out[h * SPAN : (h + 1) * SPAN]
        return 0

    lax.fori_loop(0, 8, one_block, 0)
    for d, o in enumerate((o0, o1, o2, o3)):
        o[...] = o_scr[d]


def place_kernel(where_ref, p0, p1, p2, p3, out_ref):
    x = where_ref[0]
    for d, piece in enumerate((p0, p1, p2, p3)):
        start = pl.multiple_of(lax.rem(x + d, 4) * (GROUP * HEAD), GROUP * HEAD)
        out_ref[0, :, pl.ds(start, GROUP * HEAD)] = piece[...]


def on_device(queries, keys, values, doc_lengths, interp_num, interp_den):
    bf16 = jnp.bfloat16
    where = jnp.stack([lax.axis_index(a) for a in ("x", "yh", "c")]).astype(jnp.int32)
    half = HEAD // 2
    freq = THETA ** (-(2.0 * jnp.arange(half, dtype=jnp.float32)) / HEAD)
    freq = jnp.concatenate([freq, freq])[None]
    smem = pl.BlockSpec(memory_space=pltpu.SMEM)
    vmem = pl.BlockSpec(memory_space=pltpu.VMEM)
    packed, kv = pl.pallas_call(
        pack_kernel,
        out_shape=(
            jax.ShapeDtypeStruct((4, 128, GROUP * HEAD), bf16),
            jax.ShapeDtypeStruct((16, 128, 2 * HEAD), bf16),
        ),
        in_specs=[smem] * 4 + [vmem] * 4,
        out_specs=(vmem, vmem),
        name="pack",
    )(where, doc_lengths, interp_num, interp_den, freq, queries[0], keys[0], values[0])
    pieces = [packed[0]] + [
        lax.ppermute(packed[d], AXES, route(d, 0)) for d in (1, 2, 3)
    ]
    kv = lax.all_to_all(kv, ("x", "yh"), 0, 0, tiled=True)
    twin = lax.ppermute(kv, "c", [(0, 1), (1, 0)])
    piece = jax.ShapeDtypeStruct((128, GROUP * HEAD), bf16)
    results = pl.pallas_call(
        attend_kernel,
        out_shape=(piece,) * 4,
        in_specs=[smem] * 2 + [vmem] * 6,
        out_specs=(vmem,) * 4,
        scratch_shapes=[
            pltpu.VMEM((4, 128, GROUP * HEAD), bf16),
            pltpu.VMEM((2, 16, 128, 2 * HEAD), bf16),
            pltpu.VMEM((4, 128, GROUP * HEAD), bf16),
            pltpu.VMEM((10, GROUP * SPAN, TILE), jnp.float32),
            pltpu.VMEM((GROUP * SPAN, HEAD), jnp.float32),
            pltpu.VMEM((GROUP * SPAN, 2 * HEAD), jnp.float32),
        ],
        name="attend",
    )(where, doc_lengths, *pieces, kv, twin)
    handed = [lax.ppermute(results[d], AXES, route(-d, 1)) for d in range(4)]
    return pl.pallas_call(
        place_kernel,
        out_shape=jax.ShapeDtypeStruct((1, 128, KV_HEADS * GROUP * HEAD), bf16),
        in_specs=[smem] + [vmem] * 4,
        out_specs=vmem,
        name="place",
    )(where, *handed)


def solution(mesh):
    fine = Mesh(mesh.devices.reshape(SIZES), AXES)
    ctx, section = ("x", "yh", "c"), ("yl", "z")
    placed = (
        P(section, ctx, None),
        P(section, ctx, None),
        P(section, ctx, None),
        P(section, None),
        P(),
        P(),
    )
    return jax.shard_map(
        on_device, mesh=fine, in_specs=placed, out_specs=P(section, ctx, None), check_vma=False
    )
```

```python
import functools
import math

import jax
import jax.numpy as jnp
import numpy as np
from jax import lax
from jax.experimental import pallas as pl
from jax.experimental.pallas import tpu as pltpu
from jax.sharding import Mesh, PartitionSpec as P


KV_HEADS = 4
GROUP = 8
HEAD = 128
THETA = 500000.0
MASKED = -1e30
SPAN = 64
TOKENS = 4096
TILE = 512
ROUNDS = 2112 // TILE + 1
QUERY_SCALE = math.log2(math.e) / math.sqrt(HEAD)
AXES = ("x", "yh", "c", "yl", "z")
SIZES = (4, 4, 2, 2, 12)


def route(dx, ds):
    pairs = []
    for i in range(math.prod(SIZES)):
        x, yh, c, yl, z = (int(a) for a in np.unravel_index(i, SIZES))
        s = (yl * SIZES[4] + z + ds) % (SIZES[3] * SIZES[4])
        to = ((x + dx) % 4, yh, c, s // SIZES[4], s % SIZES[4])
        pairs.append((i, int(np.ravel_multi_index(to, SIZES))))
    return pairs


def frequencies():
    half = HEAD // 2
    freq = THETA ** (-(2.0 * np.arange(half)) / HEAD)
    return np.concatenate([freq, freq]).astype(np.float32)[None]


def doc_start(position, lens_ref):
    end = 0
    start = jnp.zeros_like(position)
    for d in range(4):
        length = lens_ref[0, d]
        end = end + length
        start = start + jnp.where(position >= end, length, 0)
    return start


def pack_kernel(where_ref, lens_ref, num_ref, den_ref, freq_ref, q_ref, k_ref, v_ref, kv_ref, *q_out):
    x = where_ref[0]
    shard = x * 8 + where_ref[1] * 2 + where_ref[2]
    row = lax.broadcasted_iota(jnp.int32, (128, HEAD), 0)
    lane = lax.broadcasted_iota(jnp.int32, (128, HEAD), 1)
    position = jnp.where(row < SPAN, shard * SPAN + row, (63 - shard) * SPAN + row - SPAN)
    offset = (position - doc_start(position, lens_ref)).astype(jnp.float32)
    ratio = jnp.full((128, HEAD), num_ref[0], jnp.int32).astype(jnp.float32) / jnp.full(
        (128, HEAD), den_ref[0], jnp.int32
    ).astype(jnp.float32)
    angle = offset * ratio * freq_ref[...]
    cosine = jnp.cos(angle)
    sine = jnp.sin(angle)
    sine = jnp.where(lane < HEAD // 2, -sine, sine)
    for h in range(KV_HEADS):
        cols = slice(h * HEAD, (h + 1) * HEAD)
        wide = k_ref[:, cols].astype(jnp.float32)
        turned = (wide * cosine + pltpu.roll(wide, HEAD // 2, 1) * sine).astype(jnp.bfloat16)
        kv_ref[h, :, :HEAD] = turned
        kv_ref[h, :, HEAD:] = v_ref[:, cols]
    cosine = cosine * QUERY_SCALE
    sine = sine * QUERY_SCALE
    for d in range(4):
        group = lax.rem(x + d, 4)
        for h in range(GROUP):
            start = pl.multiple_of(group * (GROUP * HEAD) + h * HEAD, HEAD)
            wide = q_ref[:, pl.ds(start, HEAD)].astype(jnp.float32)
            turned = wide * cosine + pltpu.roll(wide, HEAD // 2, 1) * sine
            q_out[d][:, h * HEAD : (h + 1) * HEAD] = turned.astype(jnp.bfloat16)


def gather_keys(where_ref, blocks, kv_ref):
    yh, core = where_ref[1], where_ref[2]
    sides = (0, 2 * core - 1, 1 - 2 * core, 2)
    for block, side in zip(blocks, sides):
        y = lax.rem(yh + side + 4, 4)
        for c in range(2):
            for x in range(4):
                shard = x * 8 + y * 2 + c
                early = pl.multiple_of(shard * SPAN, SPAN)
                late = pl.multiple_of((63 - shard) * SPAN, SPAN)
                kv_ref[pl.ds(early, SPAN), :] = block[c, x, :SPAN, :]
                kv_ref[pl.ds(late, SPAN), :] = block[c, x, SPAN:, :]
    kv_ref[TOKENS:, :] = jnp.zeros((TILE, 2 * HEAD), jnp.bfloat16)


def attend_block(where_ref, lens_ref, dx, q_ref, kv_ref, o_ref, s_scr, m_scr, acc_scr):
    shard = lax.rem(where_ref[0] - dx + 4, 4) * 8 + where_ref[1] * 2 + where_ref[2]
    ones = jnp.ones((TILE, HEAD), jnp.bfloat16)
    row = lax.broadcasted_iota(jnp.int32, (SPAN, TILE), 0)
    lane = lax.broadcasted_iota(jnp.int32, (SPAN, TILE), 1)

    def one_half(half, _):
        rows = pl.ds(pl.multiple_of(half * SPAN, SPAN), SPAN)
        block = jnp.where(half == 0, shard, 63 - shard)
        first = block * SPAN
        low = lax.div(doc_start(first, lens_ref), SPAN) * SPAN
        count = lax.div(first - low, TILE) + 1
        q_tile = jnp.concatenate(
            [q_ref[rows, h * HEAD : (h + 1) * HEAD] for h in range(GROUP)], axis=0
        )
        q_pos = first + row
        q_start = doc_start(q_pos, lens_ref)
        m_scr[...] = jnp.full(m_scr.shape, MASKED, jnp.float32)
        acc_scr[...] = jnp.zeros_like(acc_scr)

        def scores(t, _):
            at = pl.multiple_of(low + t * TILE, SPAN)
            k_pos = at + lane
            bias = jnp.where((k_pos <= q_pos) & (k_pos >= q_start), 0.0, MASKED)
            s = lax.dot_general(
                q_tile,
                kv_ref[pl.ds(at, TILE), :HEAD],
                (((1,), (1,)), ((), ())),
                preferred_element_type=jnp.float32,
            )
            s = (s.reshape(GROUP, SPAN, TILE) + bias[None]).reshape(GROUP * SPAN, TILE)
            s_scr[t] = s
            top = m_scr[...]
            for j in range(TILE // HEAD):
                top = jnp.maximum(top, s[:, j * HEAD : (j + 1) * HEAD])
            m_scr[...] = top
            return 0

        lax.fori_loop(0, count, scores, 0)
        top = jnp.max(m_scr[...], axis=1, keepdims=True)
        m_scr[...] = jnp.broadcast_to(top, m_scr.shape)

        def weigh(t, _):
            at = pl.multiple_of(low + t * TILE, SPAN)
            m = jnp.concatenate([m_scr[...]] * (TILE // HEAD), axis=1)
            w = jnp.exp2(s_scr[t] - m).astype(jnp.bfloat16)
            v_tile = jnp.concatenate([kv_ref[pl.ds(at, TILE), HEAD:], ones], axis=1)
            acc_scr[...] += jnp.dot(w, v_tile, preferred_element_type=jnp.float32)
            return 0

        lax.fori_loop(0, count, weigh, 0)
        out = (acc_scr[:, :HEAD] / acc_scr[:, HEAD:]).astype(jnp.bfloat16)
        for h in range(GROUP):
            o_ref[rows, h * HEAD : (h + 1) * HEAD] = out[h * SPAN : (h + 1) * SPAN]
        return 0

    lax.fori_loop(0, 2, one_half, 0)


def first_kernel(dx, where_ref, lens_ref, q_ref, b0, b1, b2, b3, o_ref, kv_ref, *scratch):
    gather_keys(where_ref, (b0, b1, b2, b3), kv_ref)
    attend_block(where_ref, lens_ref, dx, q_ref, kv_ref, o_ref, *scratch)


def next_kernel(dx, where_ref, lens_ref, q_ref, kv_ref, o_ref, *scratch):
    attend_block(where_ref, lens_ref, dx, q_ref, kv_ref, o_ref, *scratch)


def place_kernel(where_ref, p0, p1, p2, p3, out_ref):
    x = where_ref[0]
    for d, piece in enumerate((p0, p1, p2, p3)):
        start = pl.multiple_of(lax.rem(x + d, 4) * (GROUP * HEAD), GROUP * HEAD)
        out_ref[0, :, pl.ds(start, GROUP * HEAD)] = piece[...]


def layer(queries, keys, values, doc_lengths, interp_num, interp_den):
    bf16 = jnp.bfloat16
    where = jnp.stack([lax.axis_index(a) for a in ("x", "yh", "c")]).astype(jnp.int32)
    smem = pl.BlockSpec(memory_space=pltpu.SMEM)
    vmem = pl.BlockSpec(memory_space=pltpu.VMEM)
    piece = jax.ShapeDtypeStruct((128, GROUP * HEAD), bf16)
    kv, *packed = pl.pallas_call(
        pack_kernel,
        out_shape=(jax.ShapeDtypeStruct((4, 128, 2 * HEAD), bf16),) + (piece,) * 4,
        in_specs=[smem] * 4 + [vmem] * 4,
        out_specs=(vmem,) * 5,
        name="pack",
    )(where, doc_lengths, interp_num, interp_den, frequencies(), queries[0], keys[0], values[0])
    kv = lax.all_to_all(kv, "x", 0, 0, tiled=True)
    near = lax.all_gather(kv, "c", axis=0)
    ring = [(y * 2 + c, (y + 1 - 2 * c) % 4 * 2 + c) for y in range(4) for c in range(2)]
    one_on = lax.ppermute(near, ("yh", "c"), ring)
    core = lax.axis_index("c")
    half = lax.dynamic_index_in_dim(one_on, core, 0, keepdims=False)
    two_on = lax.ppermute(half, ("yh", "c"), ring)
    other = lax.ppermute(one_on, "c", [(0, 1), (1, 0)])
    far = lax.all_gather(two_on, "c", axis=0)
    moved = {0: packed[0]}
    for d in (2, 1, 3):
        moved[d] = lax.ppermute(packed[d], AXES, route(d, 0))
    lengths = jnp.minimum(doc_lengths, TOKENS)
    scratch = [
        pltpu.VMEM((ROUNDS, GROUP * SPAN, TILE), jnp.float32),
        pltpu.VMEM((GROUP * SPAN, HEAD), jnp.float32),
        pltpu.VMEM((GROUP * SPAN, 2 * HEAD), jnp.float32),
    ]
    handed = {}
    ordered = None
    for d in (2, 1, 3, 0):
        if ordered is None:
            result, ordered = pl.pallas_call(
                functools.partial(first_kernel, d),
                out_shape=(piece, jax.ShapeDtypeStruct((TOKENS + TILE, 2 * HEAD), bf16)),
                in_specs=[smem] * 2 + [vmem] * 5,
                out_specs=(vmem, vmem),
                scratch_shapes=scratch,
            )(where, lengths, moved[d], near, one_on, other, far)
        else:
            result = pl.pallas_call(
                functools.partial(next_kernel, d),
                out_shape=piece,
                in_specs=[smem] * 2 + [vmem] * 2,
                out_specs=vmem,
                scratch_shapes=scratch,
            )(where, lengths, moved[d], ordered)
        handed[d] = lax.ppermute(result, AXES, route(-d, 1))
    return pl.pallas_call(
        place_kernel,
        out_shape=jax.ShapeDtypeStruct((1, 128, KV_HEADS * GROUP * HEAD), bf16),
        in_specs=[smem] + [vmem] * 4,
        out_specs=vmem,
        name="place",
    )(where, *(handed[d] for d in range(4)))


def solution(mesh):
    fine = Mesh(mesh.devices.reshape(SIZES), AXES)
    ctx, section = ("x", "yh", "c"), ("yl", "z")
    placed = (
        P(section, ctx, None),
        P(section, ctx, None),
        P(section, ctx, None),
        P(section, None),
        P(),
        P(),
    )
    return jax.shard_map(
        layer, mesh=fine, in_specs=placed, out_specs=P(section, ctx, None), check_vma=False
    )
```

```python
import functools
import math

import jax
import jax.numpy as jnp
import numpy as np
from jax import lax
from jax.experimental import pallas as pl
from jax.experimental.pallas import tpu as pltpu
from jax.sharding import Mesh, PartitionSpec as P


KV_HEADS = 4
GROUP = 8
HEAD = 128
THETA = 500000.0
MASKED = -1e30
SPAN = 64
TOKENS = 4096
TILE = 512
ROUNDS = 2176 // TILE + 1
SUMS = 16
QUERY_SCALE = math.log2(math.e) / math.sqrt(HEAD)
AXES = ("x", "yh", "c", "yl", "z")
SIZES = (4, 4, 2, 2, 12)


def route(dx, ds):
    pairs = []
    for i in range(math.prod(SIZES)):
        x, yh, c, yl, z = (int(a) for a in np.unravel_index(i, SIZES))
        s = (yl * SIZES[4] + z + ds) % (SIZES[3] * SIZES[4])
        to = ((x + dx) % 4, yh, c, s // SIZES[4], s % SIZES[4])
        pairs.append((i, int(np.ravel_multi_index(to, SIZES))))
    return pairs


def room(mib):
    return pltpu.CompilerParams(vmem_limit_bytes=mib * 2**20)


def held(x):
    return pltpu.with_memory_space_constraint(x, pltpu.VMEM)


def frequencies():
    half = HEAD // 2
    freq = THETA ** (-(2.0 * np.arange(half)) / HEAD)
    return np.concatenate([freq, freq]).astype(np.float32)[None]


def doc_start(position, lens_ref):
    end = 0
    start = jnp.zeros_like(position)
    for d in range(4):
        length = lens_ref[0, d]
        end = end + length
        start = start + jnp.where(position >= end, length, 0)
    return start


def rotation(where_ref, lens_ref, num_ref, den_ref, freq_ref, scale):
    shard = where_ref[0] * 8 + where_ref[1] * 2 + where_ref[2]
    row = lax.broadcasted_iota(jnp.int32, (128, HEAD), 0)
    lane = lax.broadcasted_iota(jnp.int32, (128, HEAD), 1)
    position = jnp.where(row < SPAN, shard * SPAN + row, (63 - shard) * SPAN + row - SPAN)
    offset = (position - doc_start(position, lens_ref)).astype(jnp.float32)
    ratio = jnp.full((128, HEAD), num_ref[0], jnp.int32).astype(jnp.float32) / jnp.full(
        (128, HEAD), den_ref[0], jnp.int32
    ).astype(jnp.float32)
    angle = offset * ratio * freq_ref[...]
    cosine = jnp.cos(angle) * scale
    sine = jnp.sin(angle) * scale
    return cosine, jnp.where(lane < HEAD // 2, -sine, sine)


def turn(part, cosine, sine):
    wide = part.astype(jnp.float32)
    return (wide * cosine + pltpu.roll(wide, HEAD // 2, 1) * sine).astype(jnp.bfloat16)


def pack_keys_kernel(where_ref, lens_ref, num_ref, den_ref, freq_ref, k_ref, v_ref, kv_ref):
    cosine, sine = rotation(where_ref, lens_ref, num_ref, den_ref, freq_ref, 1.0)
    for h in range(KV_HEADS):
        cols = slice(h * HEAD, (h + 1) * HEAD)
        kv_ref[h, :, :HEAD] = turn(k_ref[:, cols], cosine, sine)
        kv_ref[h, :, HEAD:] = v_ref[:, cols].T


def pack_queries_kernel(where_ref, lens_ref, num_ref, den_ref, freq_ref, q_ref, *q_out):
    cosine, sine = rotation(where_ref, lens_ref, num_ref, den_ref, freq_ref, QUERY_SCALE)
    for d in range(4):
        group = lax.rem(where_ref[0] + d, 4)
        for h in range(GROUP):
            start = pl.multiple_of(group * (GROUP * HEAD) + h * HEAD, HEAD)
            q_out[d][:, h * HEAD : (h + 1) * HEAD] = turn(q_ref[:, pl.ds(start, HEAD)], cosine, sine)


def gather_keys(where_ref, blocks, k_ref, vt_ref):
    yh, core = where_ref[1], where_ref[2]
    sides = (0, 2 * core - 1, 1 - 2 * core, 2)
    for block, side in zip(blocks, sides):
        y = lax.rem(yh + side + 4, 4)
        for x in range(4):
            early = pl.multiple_of((x * 8 + y * 2) * SPAN, 2 * SPAN)
            late = pl.multiple_of((62 - x * 8 - y * 2) * SPAN, 2 * SPAN)
            k_ref[pl.ds(early, 2 * SPAN), :] = jnp.concatenate(
                [block[0, x, :SPAN, :HEAD], block[1, x, :SPAN, :HEAD]], axis=0
            )
            k_ref[pl.ds(late, 2 * SPAN), :] = jnp.concatenate(
                [block[1, x, SPAN:, :HEAD], block[0, x, SPAN:, :HEAD]], axis=0
            )
            a, b = block[0, x, :, HEAD:], block[1, x, :, HEAD:]
            vt_ref[:HEAD, pl.ds(early, 2 * SPAN)] = jnp.concatenate([a[:, :SPAN], b[:, :SPAN]], axis=1)
            vt_ref[:HEAD, pl.ds(late, 2 * SPAN)] = jnp.concatenate([b[:, SPAN:], a[:, SPAN:]], axis=1)
    k_ref[TOKENS:, :] = jnp.zeros((TILE, HEAD), jnp.bfloat16)
    vt_ref[:HEAD, TOKENS:] = jnp.zeros((HEAD, TILE), jnp.bfloat16)
    vt_ref[HEAD:, :] = jnp.ones((SUMS, TOKENS + TILE), jnp.bfloat16)


def attend_block(where_ref, lens_ref, dx, q_ref, k_ref, vt_ref, o_ref, s_scr, m_scr, acc_scr):
    shard = lax.rem(where_ref[0] - dx + 4, 4) * 8 + where_ref[1] * 2 + where_ref[2]
    width = GROUP * SPAN
    key = lax.broadcasted_iota(jnp.int32, (TILE, HEAD), 0)
    token = lax.rem(lax.broadcasted_iota(jnp.int32, (8, HEAD), 1), SPAN)

    def one_half(half, _):
        rows = pl.ds(pl.multiple_of(half * SPAN, SPAN), SPAN)
        block = jnp.where(half == 0, shard, 63 - shard)
        first = block * SPAN
        low = lax.div(doc_start(first, lens_ref), HEAD) * HEAD
        count = lax.div(first - low, TILE) + 1
        q_tile = jnp.concatenate(
            [q_ref[rows, h * HEAD : (h + 1) * HEAD] for h in range(GROUP)], axis=0
        )
        q_pos = first + token
        q_start = doc_start(q_pos, lens_ref)
        m_scr[...] = jnp.full(m_scr.shape, MASKED, jnp.float32)
        acc_scr[...] = jnp.zeros_like(acc_scr)

        def scores(t, _):
            at = pl.multiple_of(low + t * TILE, HEAD)
            bias = jnp.where(
                (key <= (q_pos - at)[:1]) & (key >= (q_start - at)[:1]), 0.0, MASKED
            )
            s = lax.dot_general(
                k_ref[pl.ds(at, TILE), :],
                q_tile,
                (((1,), (1,)), ((), ())),
                preferred_element_type=jnp.float32,
            )
            s = s + jnp.concatenate([bias] * (width // HEAD), axis=1)
            s_scr[t] = s
            m_scr[...] = jnp.maximum(m_scr[...], jnp.max(s.reshape(TILE // 8, 8, width), axis=0))
            return 0

        lax.fori_loop(0, count, scores, 0)
        m_scr[...] = jnp.broadcast_to(jnp.max(m_scr[...], axis=0, keepdims=True), m_scr.shape)

        def weigh(t, _):
            at = pl.multiple_of(low + t * TILE, HEAD)
            s = s_scr[t].reshape(TILE // 8, 8, width) - m_scr[...][None]
            w = jnp.exp2(s).reshape(TILE, width).astype(jnp.bfloat16)
            acc_scr[...] += jnp.dot(
                vt_ref[:, pl.ds(at, TILE)], w, preferred_element_type=jnp.float32
            )
            return 0

        lax.fori_loop(0, count, weigh, 0)
        out = (acc_scr[:HEAD, :] * (1.0 / acc_scr[HEAD : HEAD + 1, :])).T.astype(jnp.bfloat16)
        for h in range(GROUP):
            o_ref[rows, h * HEAD : (h + 1) * HEAD] = out[h * SPAN : (h + 1) * SPAN]
        return 0

    lax.fori_loop(0, 2, one_half, 0)


def first_kernel(dx, where_ref, lens_ref, q_ref, b0, b1, b2, b3, o_ref, k_ref, vt_ref, *scratch):
    gather_keys(where_ref, (b0, b1, b2, b3), k_ref, vt_ref)
    attend_block(where_ref, lens_ref, dx, q_ref, k_ref, vt_ref, o_ref, *scratch)


def next_kernel(dx, where_ref, lens_ref, q_ref, k_ref, vt_ref, o_ref, *scratch):
    attend_block(where_ref, lens_ref, dx, q_ref, k_ref, vt_ref, o_ref, *scratch)


def first_place_kernel(col_ref, piece_ref, out_ref):
    out_ref[0] = piece_ref[...]


def next_place_kernel(col_ref, piece_ref, old_ref, out_ref):
    out_ref[0] = piece_ref[...]


def place(piece, out, column):
    width = GROUP * HEAD
    first = out is None
    return pl.pallas_call(
        first_place_kernel if first else next_place_kernel,
        out_shape=jax.ShapeDtypeStruct((1, 128, KV_HEADS * width), jnp.bfloat16),
        grid_spec=pltpu.PrefetchScalarGridSpec(
            num_scalar_prefetch=1,
            grid=(1,),
            in_specs=[pl.BlockSpec((128, width), lambda i, col: (0, 0))]
            + ([] if first else [pl.BlockSpec(memory_space=pl.ANY)]),
            out_specs=pl.BlockSpec((1, 128, width), lambda i, col: (0, 0, col[0])),
        ),
        input_output_aliases={} if first else {2: 0},
        compiler_params=room(4),
    )(*((column, held(piece)) if first else (column, held(piece), out)))


def layer(queries, keys, values, doc_lengths, interp_num, interp_den):
    bf16 = jnp.bfloat16
    where = jnp.stack([lax.axis_index(a) for a in ("x", "yh", "c")]).astype(jnp.int32)
    smem = pl.BlockSpec(memory_space=pltpu.SMEM)
    vmem = pl.BlockSpec(memory_space=pltpu.VMEM)
    piece = pltpu.VMEM((128, GROUP * HEAD), bf16)
    turning = (where, doc_lengths, interp_num, interp_den, frequencies())
    kv = pl.pallas_call(
        pack_keys_kernel,
        out_shape=pltpu.VMEM((4, 128, 2 * HEAD), bf16),
        in_specs=[smem] * 4 + [vmem] * 3,
        out_specs=vmem,
        name="pack_keys",
        compiler_params=room(12),
    )(*turning, keys[0], values[0])
    packed = pl.pallas_call(
        pack_queries_kernel,
        out_shape=(piece,) * 4,
        in_specs=[smem] * 4 + [vmem] * 2,
        out_specs=(vmem,) * 4,
        name="pack_queries",
        compiler_params=room(12),
    )(*turning, queries[0])
    kv = lax.all_to_all(kv, "x", 0, 0, tiled=True)
    near = lax.all_gather(kv, "c", axis=0)
    ring = [(y * 2 + c, (y + 1 - 2 * c) % 4 * 2 + c) for y in range(4) for c in range(2)]
    one_on = lax.ppermute(near, ("yh", "c"), ring)
    core = lax.axis_index("c")
    half = lax.dynamic_index_in_dim(one_on, core, 0, keepdims=False)
    two_on = lax.ppermute(half, ("yh", "c"), ring)
    other = lax.ppermute(one_on, "c", [(0, 1), (1, 0)])
    far = lax.all_gather(two_on, "c", axis=0)
    moved = {0: packed[0]}
    for d in (2, 1, 3):
        moved[d] = lax.ppermute(packed[d], AXES, route(d, 0))
    lengths = jnp.minimum(doc_lengths, TOKENS)
    scratch = [
        pltpu.VMEM((ROUNDS, TILE, GROUP * SPAN), jnp.float32),
        pltpu.VMEM((8, GROUP * SPAN), jnp.float32),
        pltpu.VMEM((HEAD + SUMS, GROUP * SPAN), jnp.float32),
    ]
    laid_out = (
        pltpu.VMEM((TOKENS + TILE, HEAD), bf16),
        pltpu.VMEM((HEAD + SUMS, TOKENS + TILE), bf16),
    )
    handed = {}
    ordered = None
    for d in (2, 1, 3, 0):
        if ordered is None:
            result, *ordered = pl.pallas_call(
                functools.partial(first_kernel, d),
                out_shape=(piece,) + laid_out,
                in_specs=[smem] * 2 + [vmem] * 5,
                out_specs=(vmem,) * 3,
                scratch_shapes=scratch,
                compiler_params=room(24),
            )(where, lengths, *map(held, (moved[d], near, one_on, other, far)))
        else:
            result = pl.pallas_call(
                functools.partial(next_kernel, d),
                out_shape=piece,
                in_specs=[smem] * 2 + [vmem] * 3,
                out_specs=vmem,
                scratch_shapes=scratch,
                compiler_params=room(24),
            )(where, lengths, *map(held, (moved[d], *ordered)))
        handed[d] = lax.ppermute(result, AXES, route(-d, 1))
    out = None
    for d in (2, 1, 3, 0):
        out = place(handed[d], out, (where[:1] + d) % 4)
    return out


def solution(mesh):
    fine = Mesh(mesh.devices.reshape(SIZES), AXES)
    ctx, section = ("x", "yh", "c"), ("yl", "z")
    placed = (
        P(section, ctx, None),
        P(section, ctx, None),
        P(section, ctx, None),
        P(section, None),
        P(),
        P(),
    )
    return jax.shard_map(
        layer, mesh=fine, in_specs=placed, out_specs=P(section, ctx, None), check_vma=False
    )
```

```python
import functools
import math

import jax
import jax.numpy as jnp
import numpy as np
from jax import lax
from jax.experimental import pallas as pl
from jax.experimental.pallas import tpu as pltpu
from jax.sharding import Mesh, PartitionSpec as P


KV_HEADS = 4
GROUP = 8
HEAD = 128
THETA = 500000.0
MASKED = -1e30
SPAN = 64
TOKENS = 4096
TILE = 512
ROUNDS = 2176 // TILE + 1
SUMS = 16
QUERY_SCALE = math.log2(math.e) / math.sqrt(HEAD)
AXES = ("x", "yh", "c", "yl", "z")
SIZES = (4, 4, 2, 2, 12)


def route(dx, ds):
    pairs = []
    for i in range(math.prod(SIZES)):
        x, yh, c, yl, z = (int(a) for a in np.unravel_index(i, SIZES))
        s = (yl * SIZES[4] + z + ds) % (SIZES[3] * SIZES[4])
        to = ((x + dx) % 4, yh, c, s // SIZES[4], s % SIZES[4])
        pairs.append((i, int(np.ravel_multi_index(to, SIZES))))
    return pairs


def room(mib):
    return pltpu.CompilerParams(vmem_limit_bytes=mib * 2**20)


def held(x):
    return pltpu.with_memory_space_constraint(x, pltpu.VMEM)


def in_hbm(x):
    return pltpu.with_memory_space_constraint(x, pltpu.HBM)


def frequencies():
    half = HEAD // 2
    freq = THETA ** (-(2.0 * np.arange(half)) / HEAD)
    return np.concatenate([freq, freq]).astype(np.float32)[None]


LENGTHS, NUMERATOR, DENOMINATOR = 3, 7, 8


def doc_start(position, scalars):
    end = 0
    start = jnp.zeros_like(position)
    for d in range(4):
        length = scalars[LENGTHS + d]
        end = end + length
        start = start + jnp.where(position >= end, length, 0)
    return start


def rotation(scalars, freq_ref, scale):
    shard = scalars[0] * 8 + scalars[1] * 2 + scalars[2]
    row = lax.broadcasted_iota(jnp.int32, (128, HEAD), 0)
    lane = lax.broadcasted_iota(jnp.int32, (128, HEAD), 1)
    position = jnp.where(row < SPAN, shard * SPAN + row, (63 - shard) * SPAN + row - SPAN)
    offset = (position - doc_start(position, scalars)).astype(jnp.float32)
    ratio = jnp.full((128, HEAD), scalars[NUMERATOR], jnp.int32).astype(jnp.float32) / jnp.full(
        (128, HEAD), scalars[DENOMINATOR], jnp.int32
    ).astype(jnp.float32)
    angle = offset * ratio * freq_ref[...]
    cosine = jnp.cos(angle) * scale
    sine = jnp.sin(angle) * scale
    return cosine, jnp.where(lane < HEAD // 2, -sine, sine)


def turn(part, cosine, sine):
    wide = part.astype(jnp.float32)
    return (wide * cosine + pltpu.roll(wide, HEAD // 2, 1) * sine).astype(jnp.bfloat16)


def pack_keys_kernel(scalars, freq_ref, k_ref, v_ref, kv_ref):
    cosine, sine = rotation(scalars, freq_ref, 1.0)
    for h in range(KV_HEADS):
        cols = slice(h * HEAD, (h + 1) * HEAD)
        kv_ref[h, :, :HEAD] = turn(k_ref[:, cols], cosine, sine)
        kv_ref[h, :, HEAD:] = v_ref[:, cols].T


def pack_queries_kernel(scalars, freq_ref, q_ref, *q_out):
    cosine, sine = rotation(scalars, freq_ref, QUERY_SCALE)
    for d in range(4):
        group = lax.rem(scalars[0] + d, 4)
        for h in range(GROUP):
            start = pl.multiple_of(group * (GROUP * HEAD) + h * HEAD, HEAD)
            q_out[d][:, h * HEAD : (h + 1) * HEAD] = turn(q_ref[:, pl.ds(start, HEAD)], cosine, sine)


def gather_keys(scalars, blocks, k_ref, vt_ref):
    yh, core = scalars[1], scalars[2]
    sides = (0, 2 * core - 1, 1 - 2 * core, 2)
    for (mine, others), side in zip(blocks, sides):
        y = lax.rem(yh + side + 4, 4)
        for x in range(4):
            early = pl.multiple_of((x * 8 + y * 2) * SPAN, 2 * SPAN)
            late = pl.multiple_of((62 - x * 8 - y * 2) * SPAN, 2 * SPAN)
            m, o = mine[x], others[x]
            zero, one = jnp.where(core == 0, m, o), jnp.where(core == 0, o, m)
            k_ref[pl.ds(early, 2 * SPAN), :] = jnp.concatenate(
                [zero[:SPAN, :HEAD], one[:SPAN, :HEAD]], axis=0
            )
            k_ref[pl.ds(late, 2 * SPAN), :] = jnp.concatenate(
                [one[SPAN:, :HEAD], zero[SPAN:, :HEAD]], axis=0
            )
            a, b = zero[:, HEAD:], one[:, HEAD:]
            vt_ref[:HEAD, pl.ds(early, 2 * SPAN)] = jnp.concatenate([a[:, :SPAN], b[:, :SPAN]], axis=1)
            vt_ref[:HEAD, pl.ds(late, 2 * SPAN)] = jnp.concatenate([b[:, SPAN:], a[:, SPAN:]], axis=1)
    k_ref[TOKENS:, :] = jnp.zeros((TILE, HEAD), jnp.bfloat16)
    vt_ref[:HEAD, TOKENS:] = jnp.zeros((HEAD, TILE), jnp.bfloat16)
    vt_ref[HEAD:, :] = jnp.ones((SUMS, TOKENS + TILE), jnp.bfloat16)


def attend_block(scalars, dx, q_ref, k_ref, vt_ref, o_ref, s_scr, m_scr, acc_scr):
    shard = lax.rem(scalars[0] - dx + 4, 4) * 8 + scalars[1] * 2 + scalars[2]
    width = GROUP * SPAN
    key = lax.broadcasted_iota(jnp.int32, (TILE, HEAD), 0)
    token = lax.rem(lax.broadcasted_iota(jnp.int32, (8, HEAD), 1), SPAN)

    def one_half(half, _):
        rows = pl.ds(pl.multiple_of(half * SPAN, SPAN), SPAN)
        block = jnp.where(half == 0, shard, 63 - shard)
        first = block * SPAN
        low = lax.div(doc_start(first, scalars), HEAD) * HEAD
        count = lax.div(first - low, TILE) + 1
        q_tile = jnp.concatenate(
            [q_ref[rows, h * HEAD : (h + 1) * HEAD] for h in range(GROUP)], axis=0
        )
        q_pos = first + token
        q_start = doc_start(q_pos, scalars)
        m_scr[...] = jnp.full(m_scr.shape, MASKED, jnp.float32)
        acc_scr[...] = jnp.zeros_like(acc_scr)

        def scores(t, _):
            at = pl.multiple_of(low + t * TILE, HEAD)
            bias = jnp.where(
                (key <= (q_pos - at)[:1]) & (key >= (q_start - at)[:1]), 0.0, MASKED
            )
            s = lax.dot_general(
                k_ref[pl.ds(at, TILE), :],
                q_tile,
                (((1,), (1,)), ((), ())),
                preferred_element_type=jnp.float32,
            )
            s = s + jnp.concatenate([bias] * (width // HEAD), axis=1)
            s_scr[t] = s
            m_scr[...] = jnp.maximum(m_scr[...], jnp.max(s.reshape(TILE // 8, 8, width), axis=0))
            return 0

        lax.fori_loop(0, count, scores, 0)
        m_scr[...] = jnp.broadcast_to(jnp.max(m_scr[...], axis=0, keepdims=True), m_scr.shape)

        def weigh(t, _):
            at = pl.multiple_of(low + t * TILE, HEAD)
            s = s_scr[t].reshape(TILE // 8, 8, width) - m_scr[...][None]
            w = jnp.exp2(s).reshape(TILE, width).astype(jnp.bfloat16)
            acc_scr[...] += jnp.dot(
                vt_ref[:, pl.ds(at, TILE)], w, preferred_element_type=jnp.float32
            )
            return 0

        lax.fori_loop(0, count, weigh, 0)
        out = (acc_scr[:HEAD, :] * (1.0 / acc_scr[HEAD : HEAD + 1, :])).T.astype(jnp.bfloat16)
        for h in range(GROUP):
            o_ref[rows, h * HEAD : (h + 1) * HEAD] = out[h * SPAN : (h + 1) * SPAN]
        return 0

    lax.fori_loop(0, 2, one_half, 0)


def first_kernel(dx, scalars, q_ref, *refs):
    halves, (o_ref, k_ref, vt_ref), scratch = refs[:8], refs[8:11], refs[11:]
    gather_keys(scalars, [halves[i : i + 2] for i in range(0, 8, 2)], k_ref, vt_ref)
    attend_block(scalars, dx, q_ref, k_ref, vt_ref, o_ref, *scratch)


def next_kernel(dx, scalars, q_ref, k_ref, vt_ref, o_ref, *scratch):
    attend_block(scalars, dx, q_ref, k_ref, vt_ref, o_ref, *scratch)


def first_place_kernel(col_ref, piece_ref, out_ref):
    out_ref[0] = piece_ref[...]


def next_place_kernel(col_ref, piece_ref, old_ref, out_ref):
    out_ref[0] = piece_ref[...]


def place(piece, out, column):
    width = GROUP * HEAD
    first = out is None
    return pl.pallas_call(
        first_place_kernel if first else next_place_kernel,
        out_shape=jax.ShapeDtypeStruct((1, 128, KV_HEADS * width), jnp.bfloat16),
        grid_spec=pltpu.PrefetchScalarGridSpec(
            num_scalar_prefetch=1,
            grid=(1,),
            in_specs=[pl.BlockSpec((128, width), lambda i, col: (0, 0))]
            + ([] if first else [pl.BlockSpec(memory_space=pl.ANY)]),
            out_specs=pl.BlockSpec((1, 128, width), lambda i, col: (0, 0, col[0])),
        ),
        input_output_aliases={} if first else {2: 0},
        compiler_params=room(4),
    )(*((column, held(piece)) if first else (column, held(piece), out)))


def layer(queries, keys, values, doc_lengths, interp_num, interp_den):
    bf16 = jnp.bfloat16
    place_in = jnp.stack([lax.axis_index(a) for a in ("x", "yh", "c")]).astype(jnp.int32)
    scalars = jnp.concatenate([place_in, doc_lengths[0], interp_num, interp_den])
    smem = pl.BlockSpec(memory_space=pltpu.SMEM)
    vmem = pl.BlockSpec(memory_space=pltpu.VMEM)
    piece = pltpu.VMEM((128, GROUP * HEAD), bf16)
    freq = in_hbm(jnp.asarray(frequencies()))
    kv = pl.pallas_call(
        pack_keys_kernel,
        out_shape=pltpu.VMEM((4, 128, 2 * HEAD), bf16),
        in_specs=[smem] + [vmem] * 3,
        out_specs=vmem,
        name="pack_keys",
        compiler_params=room(12),
    )(scalars, freq, in_hbm(keys[0]), in_hbm(values[0]))
    packed = pl.pallas_call(
        pack_queries_kernel,
        out_shape=(piece,) * 4,
        in_specs=[smem] + [vmem] * 2,
        out_specs=(vmem,) * 4,
        name="pack_queries",
        compiler_params=room(12),
    )(scalars, freq, queries[0])
    mine = lax.all_to_all(kv, "x", 0, 0, tiled=True)
    swap_cores = functools.partial(lax.ppermute, axis_name="c", perm=[(0, 1), (1, 0)])
    ring = [(y * 2 + c, (y + 1 - 2 * c) % 4 * 2 + c) for y in range(4) for c in range(2)]
    pass_on = functools.partial(lax.ppermute, axis_name=("yh", "c"), perm=ring)
    near_mine = pass_on(mine)
    twin = swap_cores(mine)
    near_twin = pass_on(twin)
    far_mine = pass_on(near_mine)
    other_a = swap_cores(near_mine)
    other_b = swap_cores(near_twin)
    far_twin = swap_cores(far_mine)
    halves = (mine, twin, near_mine, near_twin, other_b, other_a, far_mine, far_twin)
    moved = {0: packed[0]}
    for d in (2, 1, 3):
        moved[d] = lax.ppermute(packed[d], AXES, route(d, 0))
    marked = jnp.minimum(scalars, TOKENS)
    scratch = [
        pltpu.VMEM((ROUNDS, TILE, GROUP * SPAN), jnp.float32),
        pltpu.VMEM((8, GROUP * SPAN), jnp.float32),
        pltpu.VMEM((HEAD + SUMS, GROUP * SPAN), jnp.float32),
    ]
    laid_out = (
        pltpu.VMEM((TOKENS + TILE, HEAD), bf16),
        pltpu.VMEM((HEAD + SUMS, TOKENS + TILE), bf16),
    )
    handed = {}
    ordered = None
    for d in (2, 1, 3, 0):
        if ordered is None:
            result, *ordered = pl.pallas_call(
                functools.partial(first_kernel, d),
                out_shape=(piece,) + laid_out,
                in_specs=[smem] + [vmem] * 9,
                out_specs=(vmem,) * 3,
                scratch_shapes=scratch,
                compiler_params=room(24),
            )(marked, *map(held, (moved[d], *halves)))
        else:
            result = pl.pallas_call(
                functools.partial(next_kernel, d),
                out_shape=piece,
                in_specs=[smem] + [vmem] * 3,
                out_specs=vmem,
                scratch_shapes=scratch,
                compiler_params=room(24),
            )(marked, *map(held, (moved[d], *ordered)))
        handed[d] = lax.ppermute(result, AXES, route(-d, 1))
    out = None
    for d in (2, 1, 3, 0):
        out = place(handed[d], out, (marked[:1] + d) % 4)
    return out


def solution(mesh):
    fine = Mesh(mesh.devices.reshape(SIZES), AXES)
    ctx, section = ("x", "yh", "c"), ("yl", "z")
    placed = (
        P(section, ctx, None),
        P(section, ctx, None),
        P(section, ctx, None),
        P(section, None),
        P(),
        P(),
    )
    return jax.shard_map(
        layer, mesh=fine, in_specs=placed, out_specs=P(section, ctx, None), check_vma=False
    )
```

```python
import functools
import math

import jax
import jax.numpy as jnp
import numpy as np
from jax import lax
from jax.experimental import pallas as pl
from jax.experimental.pallas import tpu as pltpu
from jax.sharding import Mesh, PartitionSpec as P


KV_HEADS = 4
GROUP = 8
HEAD = 128
THETA = 500000.0
MASKED = -1e30
SPAN = 64
TOKENS = 4096
CALLS = ((2,), (1,), (3,), (0,))
TILE = 512
ROUNDS = 2176 // TILE + 1
SUMS = 16
QUERY_SCALE = math.log2(math.e) / math.sqrt(HEAD)
AXES = ("x", "yh", "c", "yl", "z")
SIZES = (4, 4, 2, 2, 12)


def route(dx, ds):
    pairs = []
    for i in range(math.prod(SIZES)):
        x, yh, c, yl, z = (int(a) for a in np.unravel_index(i, SIZES))
        s = (yl * SIZES[4] + z + ds) % (SIZES[3] * SIZES[4])
        to = ((x + dx) % 4, yh, c, s // SIZES[4], s % SIZES[4])
        pairs.append((i, int(np.ravel_multi_index(to, SIZES))))
    return pairs


def room(mib):
    return pltpu.CompilerParams(vmem_limit_bytes=mib * 2**20)


def held(x):
    return pltpu.with_memory_space_constraint(x, pltpu.VMEM)


def in_hbm(x):
    return pltpu.with_memory_space_constraint(x, pltpu.HBM)


def frequencies():
    half = HEAD // 2
    freq = THETA ** (-(2.0 * np.arange(half)) / HEAD)
    return np.concatenate([freq, freq]).astype(np.float32)[None]


LENGTHS, NUMERATOR, DENOMINATOR = 3, 7, 8


def doc_start(position, scalars):
    end = 0
    start = jnp.zeros_like(position)
    for d in range(4):
        length = scalars[LENGTHS + d]
        end = end + length
        start = start + jnp.where(position >= end, length, 0)
    return start


def rotation(scalars, freq_ref, scale):
    shard = scalars[0] * 8 + scalars[1] * 2 + scalars[2]
    row = lax.broadcasted_iota(jnp.int32, (128, HEAD), 0)
    lane = lax.broadcasted_iota(jnp.int32, (128, HEAD), 1)
    position = jnp.where(row < SPAN, shard * SPAN + row, (63 - shard) * SPAN + row - SPAN)
    offset = (position - doc_start(position, scalars)).astype(jnp.float32)
    ratio = jnp.full((128, HEAD), scalars[NUMERATOR], jnp.int32).astype(jnp.float32) / jnp.full(
        (128, HEAD), scalars[DENOMINATOR], jnp.int32
    ).astype(jnp.float32)
    angle = offset * ratio * freq_ref[...]
    cosine = jnp.cos(angle) * scale
    sine = jnp.sin(angle) * scale
    return cosine, jnp.where(lane < HEAD // 2, -sine, sine)


def turn(part, cosine, sine):
    wide = part.astype(jnp.float32)
    return (wide * cosine + pltpu.roll(wide, HEAD // 2, 1) * sine).astype(jnp.bfloat16)


def pack_keys_kernel(scalars, freq_ref, k_ref, v_ref, kv_ref):
    cosine, sine = rotation(scalars, freq_ref, 1.0)
    for h in range(KV_HEADS):
        cols = slice(h * HEAD, (h + 1) * HEAD)
        kv_ref[h, :, :HEAD] = turn(k_ref[:, cols], cosine, sine)
        kv_ref[h, :, HEAD:] = v_ref[:, cols].T


def pack_queries_kernel(scalars, freq_ref, q_ref, *q_out):
    cosine, sine = rotation(scalars, freq_ref, QUERY_SCALE)
    for d in range(4):
        group = lax.rem(scalars[0] + d, 4)
        for h in range(GROUP):
            start = pl.multiple_of(group * (GROUP * HEAD) + h * HEAD, HEAD)
            q_out[d][:, h * HEAD : (h + 1) * HEAD] = turn(q_ref[:, pl.ds(start, HEAD)], cosine, sine)


def gather_keys(scalars, blocks, k_ref, vt_ref):
    yh, core = scalars[1], scalars[2]
    sides = (0, 2 * core - 1, 1 - 2 * core, 2)
    for (mine, others), side in zip(blocks, sides):
        y = lax.rem(yh + side + 4, 4)
        for x in range(4):
            early = pl.multiple_of((x * 8 + y * 2) * SPAN, 2 * SPAN)
            late = pl.multiple_of((62 - x * 8 - y * 2) * SPAN, 2 * SPAN)
            m, o = mine[x], others[x]
            zero, one = jnp.where(core == 0, m, o), jnp.where(core == 0, o, m)
            k_ref[pl.ds(early, 2 * SPAN), :] = jnp.concatenate(
                [zero[:SPAN, :HEAD], one[:SPAN, :HEAD]], axis=0
            )
            k_ref[pl.ds(late, 2 * SPAN), :] = jnp.concatenate(
                [one[SPAN:, :HEAD], zero[SPAN:, :HEAD]], axis=0
            )
            a, b = zero[:, HEAD:], one[:, HEAD:]
            vt_ref[:HEAD, pl.ds(early, 2 * SPAN)] = jnp.concatenate([a[:, :SPAN], b[:, :SPAN]], axis=1)
            vt_ref[:HEAD, pl.ds(late, 2 * SPAN)] = jnp.concatenate([b[:, SPAN:], a[:, SPAN:]], axis=1)
    k_ref[TOKENS:, :] = jnp.zeros((TILE, HEAD), jnp.bfloat16)
    vt_ref[:HEAD, TOKENS:] = jnp.zeros((HEAD, TILE), jnp.bfloat16)
    vt_ref[HEAD:, :] = jnp.ones((SUMS, TOKENS + TILE), jnp.bfloat16)


def attend_block(scalars, dx, q_ref, k_ref, vt_ref, o_ref, s_scr, m_scr, acc_scr):
    shard = lax.rem(scalars[0] - dx + 4, 4) * 8 + scalars[1] * 2 + scalars[2]
    width = GROUP * SPAN
    key = lax.broadcasted_iota(jnp.int32, (TILE, HEAD), 0)
    token = lax.rem(lax.broadcasted_iota(jnp.int32, (8, HEAD), 1), SPAN)

    def one_half(half, _):
        rows = pl.ds(pl.multiple_of(half * SPAN, SPAN), SPAN)
        block = jnp.where(half == 0, shard, 63 - shard)
        first = block * SPAN
        low = lax.div(doc_start(first, scalars), HEAD) * HEAD
        count = lax.div(first - low, TILE) + 1
        q_tile = jnp.concatenate(
            [q_ref[rows, h * HEAD : (h + 1) * HEAD] for h in range(GROUP)], axis=0
        )
        q_pos = first + token
        q_start = doc_start(q_pos, scalars)
        m_scr[...] = jnp.full(m_scr.shape, MASKED, jnp.float32)
        acc_scr[...] = jnp.zeros_like(acc_scr)

        def scores(t, tiles):
            top = m_scr[...]
            for u in range(tiles):
                at = pl.multiple_of(low + (t + u) * TILE, HEAD)
                bias = jnp.where(
                    (key <= (q_pos - at)[:1]) & (key >= (q_start - at)[:1]), 0.0, MASKED
                )
                s = lax.dot_general(
                    k_ref[pl.ds(at, TILE), :],
                    q_tile,
                    (((1,), (1,)), ((), ())),
                    preferred_element_type=jnp.float32,
                )
                s = s + jnp.concatenate([bias] * (width // HEAD), axis=1)
                s_scr[t + u] = s
                top = jnp.maximum(top, jnp.max(s.reshape(TILE // 8, 8, width), axis=0))
            m_scr[...] = top

        def weigh(t, tiles):
            weights = []
            for u in range(tiles):
                s = s_scr[t + u].reshape(TILE // 8, 8, width) - m_scr[...][None]
                weights.append(jnp.exp2(s).reshape(TILE, width).astype(jnp.bfloat16))
            at = pl.multiple_of(low + t * TILE, HEAD)
            acc_scr[...] += jnp.dot(
                vt_ref[:, pl.ds(at, tiles * TILE)],
                jnp.concatenate(weights, axis=0),
                preferred_element_type=jnp.float32,
            )

        def in_pairs(step):
            def pair(i, _):
                step(2 * i, 2)
                return 0

            lax.fori_loop(0, lax.div(count, 2), pair, 0)
            pl.when(lax.rem(count, 2) == 1)(lambda: step(count - 1, 1))

        in_pairs(scores)
        m_scr[...] = jnp.broadcast_to(jnp.max(m_scr[...], axis=0, keepdims=True), m_scr.shape)
        in_pairs(weigh)
        out = (acc_scr[:HEAD, :] * (1.0 / acc_scr[HEAD : HEAD + 1, :])).T.astype(jnp.bfloat16)
        for h in range(GROUP):
            o_ref[rows, h * HEAD : (h + 1) * HEAD] = out[h * SPAN : (h + 1) * SPAN]
        return 0

    lax.fori_loop(0, 2, one_half, 0)


def first_kernel(dxs, scalars, *refs):
    n = len(dxs)
    queries, halves, outs, (k_ref, vt_ref) = refs[:n], refs[n : n + 8], refs[n + 8 : 2 * n + 8], refs[2 * n + 8 : 2 * n + 10]
    gather_keys(scalars, [halves[i : i + 2] for i in range(0, 8, 2)], k_ref, vt_ref)
    for dx, q_ref, o_ref in zip(dxs, queries, outs):
        attend_block(scalars, dx, q_ref, k_ref, vt_ref, o_ref, *refs[2 * n + 10 :])


def next_kernel(dxs, scalars, *refs):
    n = len(dxs)
    queries, (k_ref, vt_ref), outs = refs[:n], refs[n : n + 2], refs[n + 2 : 2 * n + 2]
    for dx, q_ref, o_ref in zip(dxs, queries, outs):
        attend_block(scalars, dx, q_ref, k_ref, vt_ref, o_ref, *refs[2 * n + 2 :])


def first_place_kernel(col_ref, piece_ref, out_ref):
    out_ref[0] = piece_ref[...]


def next_place_kernel(col_ref, piece_ref, old_ref, out_ref):
    out_ref[0] = piece_ref[...]


def place(piece, out, column):
    width = GROUP * HEAD
    first = out is None
    return pl.pallas_call(
        first_place_kernel if first else next_place_kernel,
        out_shape=jax.ShapeDtypeStruct((1, 128, KV_HEADS * width), jnp.bfloat16),
        grid_spec=pltpu.PrefetchScalarGridSpec(
            num_scalar_prefetch=1,
            grid=(1,),
            in_specs=[pl.BlockSpec((128, width), lambda i, col: (0, 0))]
            + ([] if first else [pl.BlockSpec(memory_space=pl.ANY)]),
            out_specs=pl.BlockSpec((1, 128, width), lambda i, col: (0, 0, col[0])),
        ),
        input_output_aliases={} if first else {2: 0},
        compiler_params=room(4),
    )(*((column, held(piece)) if first else (column, held(piece), out)))


def layer(queries, keys, values, doc_lengths, interp_num, interp_den):
    bf16 = jnp.bfloat16
    place_in = jnp.stack([lax.axis_index(a) for a in ("x", "yh", "c")]).astype(jnp.int32)
    scalars = jnp.concatenate([place_in, doc_lengths[0], interp_num, interp_den])
    smem = pl.BlockSpec(memory_space=pltpu.SMEM)
    vmem = pl.BlockSpec(memory_space=pltpu.VMEM)
    piece = pltpu.VMEM((128, GROUP * HEAD), bf16)
    freq = in_hbm(jnp.asarray(frequencies()))
    kv = pl.pallas_call(
        pack_keys_kernel,
        out_shape=pltpu.VMEM((4, 128, 2 * HEAD), bf16),
        in_specs=[smem] + [vmem] * 3,
        out_specs=vmem,
        name="pack_keys",
        compiler_params=room(12),
    )(scalars, freq, in_hbm(keys[0]), in_hbm(values[0]))
    packed = pl.pallas_call(
        pack_queries_kernel,
        out_shape=(piece,) * 4,
        in_specs=[smem] + [vmem] * 2,
        out_specs=(vmem,) * 4,
        name="pack_queries",
        compiler_params=room(12),
    )(scalars, freq, queries[0])
    mine = lax.all_to_all(kv, "x", 0, 0, tiled=True)
    swap_cores = functools.partial(lax.ppermute, axis_name="c", perm=[(0, 1), (1, 0)])
    ring = [(y * 2 + c, (y + 1 - 2 * c) % 4 * 2 + c) for y in range(4) for c in range(2)]
    pass_on = functools.partial(lax.ppermute, axis_name=("yh", "c"), perm=ring)
    near_mine = pass_on(mine)
    twin = swap_cores(mine)
    near_twin = pass_on(twin)
    far_mine = pass_on(near_mine)
    other_a = swap_cores(near_mine)
    other_b = swap_cores(near_twin)
    far_twin = swap_cores(far_mine)
    halves = (mine, twin, near_mine, near_twin, other_b, other_a, far_mine, far_twin)
    moved = {0: packed[0]}
    for d in (2, 1, 3):
        moved[d] = lax.ppermute(packed[d], AXES, route(d, 0))
    marked = jnp.minimum(scalars, TOKENS)
    scratch = [
        pltpu.VMEM((ROUNDS, TILE, GROUP * SPAN), jnp.float32),
        pltpu.VMEM((8, GROUP * SPAN), jnp.float32),
        pltpu.VMEM((HEAD + SUMS, GROUP * SPAN), jnp.float32),
    ]
    laid_out = (
        pltpu.VMEM((TOKENS + TILE, HEAD), bf16),
        pltpu.VMEM((HEAD + SUMS, TOKENS + TILE), bf16),
    )
    handed = {}
    ordered = None
    for dxs in CALLS:
        n = len(dxs)
        if ordered is None:
            *results, key_rows, value_columns = pl.pallas_call(
                functools.partial(first_kernel, dxs),
                out_shape=(piece,) * n + laid_out,
                in_specs=[smem] + [vmem] * (n + 8),
                out_specs=(vmem,) * (n + 2),
                scratch_shapes=scratch,
                compiler_params=room(24),
            )(marked, *map(held, [moved[d] for d in dxs]), *map(held, halves))
            ordered = (key_rows, value_columns)
        else:
            results = pl.pallas_call(
                functools.partial(next_kernel, dxs),
                out_shape=(piece,) * n,
                in_specs=[smem] + [vmem] * (n + 2),
                out_specs=(vmem,) * n,
                scratch_shapes=scratch,
                compiler_params=room(24),
            )(marked, *map(held, [moved[d] for d in dxs]), *map(held, ordered))
        for d, result in zip(dxs, results):
            handed[d] = lax.ppermute(result, AXES, route(-d, 1))
    out = None
    for d in sum(CALLS, ()):
        out = place(handed[d], out, (marked[:1] + d) % 4)
    return out


def solution(mesh):
    fine = Mesh(mesh.devices.reshape(SIZES), AXES)
    ctx, section = ("x", "yh", "c"), ("yl", "z")
    placed = (
        P(section, ctx, None),
        P(section, ctx, None),
        P(section, ctx, None),
        P(section, None),
        P(),
        P(),
    )
    return jax.shard_map(
        layer, mesh=fine, in_specs=placed, out_specs=P(section, ctx, None), check_vma=False
    )
```

```python
import functools
import math

import jax
import jax.numpy as jnp
import numpy as np
from jax import lax
from jax.experimental import pallas as pl
from jax.experimental.pallas import tpu as pltpu
from jax.sharding import Mesh, PartitionSpec as P


KV_HEADS = 4
GROUP = 8
HEAD = 128
THETA = 500000.0
MASKED = -1e30
SPAN = 64
TOKENS = 4096
CALLS = ((2,), (1,), (3,), (0,))
TILE = 512
ROUNDS = 2176 // TILE + 1
SUMS = 16
QUERY_SCALE = math.log2(math.e) / math.sqrt(HEAD)
AXES = ("x", "yh", "c", "yl", "z")
SIZES = (4, 4, 2, 2, 12)


def route(dx, ds):
    pairs = []
    for i in range(math.prod(SIZES)):
        x, yh, c, yl, z = (int(a) for a in np.unravel_index(i, SIZES))
        s = (yl * SIZES[4] + z + ds) % (SIZES[3] * SIZES[4])
        to = ((x + dx) % 4, yh, c, s // SIZES[4], s % SIZES[4])
        pairs.append((i, int(np.ravel_multi_index(to, SIZES))))
    return pairs


def room(mib):
    return pltpu.CompilerParams(vmem_limit_bytes=mib * 2**20)


def held(x):
    return pltpu.with_memory_space_constraint(x, pltpu.VMEM)


def in_hbm(x):
    return pltpu.with_memory_space_constraint(x, pltpu.HBM)


def frequencies():
    half = HEAD // 2
    freq = THETA ** (-(2.0 * np.arange(half)) / HEAD)
    return np.concatenate([freq, freq]).astype(np.float32)[None]


LENGTHS, NUMERATOR, DENOMINATOR = 3, 7, 8


def lengths_of(scalars):
    return [scalars[LENGTHS + d] for d in range(4)]


def doc_start(position, lengths):
    end = 0
    start = jnp.zeros_like(position)
    for length in lengths:
        end = end + length
        start = start + jnp.where(position >= end, length, 0)
    return start


def rotation(shard, lengths, ratio, freq_ref, scale):
    row = lax.broadcasted_iota(jnp.int32, (128, HEAD), 0)
    lane = lax.broadcasted_iota(jnp.int32, (128, HEAD), 1)
    position = jnp.where(row < SPAN, shard * SPAN + row, (63 - shard) * SPAN + row - SPAN)
    offset = (position - doc_start(position, lengths)).astype(jnp.float32)
    angle = offset * ratio * freq_ref[...]
    cosine = jnp.cos(angle) * scale
    sine = jnp.sin(angle) * scale
    return cosine, jnp.where(lane < HEAD // 2, -sine, sine)


def ratio_of(numerator, denominator):
    top = jnp.full((128, HEAD), numerator, jnp.int32).astype(jnp.float32)
    return top / jnp.full((128, HEAD), denominator, jnp.int32).astype(jnp.float32)


def turn(part, cosine, sine):
    wide = part.astype(jnp.float32)
    return (wide * cosine + pltpu.roll(wide, HEAD // 2, 1) * sine).astype(jnp.bfloat16)


def pack_keys_kernel(lengths_ref, num_ref, den_ref, freq_ref, k_ref, v_ref, kv_ref):
    shard = lax.axis_index("x") * 8 + lax.axis_index("yh") * 2 + lax.axis_index("c")
    lengths = [lengths_ref[0, d] for d in range(4)]
    cosine, sine = rotation(shard, lengths, ratio_of(num_ref[0], den_ref[0]), freq_ref, 1.0)
    for h in range(KV_HEADS):
        cols = slice(h * HEAD, (h + 1) * HEAD)
        kv_ref[h, :, :HEAD] = turn(k_ref[:, cols], cosine, sine)
        kv_ref[h, :, HEAD:] = v_ref[:, cols].T


def pack_queries_kernel(scalars, freq_ref, q_ref, *q_out):
    shard = scalars[0] * 8 + scalars[1] * 2 + scalars[2]
    ratio = ratio_of(scalars[NUMERATOR], scalars[DENOMINATOR])
    cosine, sine = rotation(shard, lengths_of(scalars), ratio, freq_ref, QUERY_SCALE)
    for d in range(4):
        group = lax.rem(scalars[0] + d, 4)
        for h in range(GROUP):
            start = pl.multiple_of(group * (GROUP * HEAD) + h * HEAD, HEAD)
            q_out[d][:, h * HEAD : (h + 1) * HEAD] = turn(q_ref[:, pl.ds(start, HEAD)], cosine, sine)


def gather_keys(scalars, halves, far_ref, k_ref, vt_ref):
    yh, core = scalars[1], scalars[2]
    sides = (0, 2 * core - 1, 1 - 2 * core, 2)
    for g, side in enumerate(sides):
        y = lax.rem(yh + side + 4, 4)
        for x in range(4):
            early = pl.multiple_of((x * 8 + y * 2) * SPAN, 2 * SPAN)
            late = pl.multiple_of((62 - x * 8 - y * 2) * SPAN, 2 * SPAN)
            if g == 3:
                zero, one = far_ref[0, x], far_ref[1, x]
            else:
                m, o = halves[2 * g][x], halves[2 * g + 1][x]
                zero, one = jnp.where(core == 0, m, o), jnp.where(core == 0, o, m)
            k_ref[pl.ds(early, 2 * SPAN), :] = jnp.concatenate(
                [zero[:SPAN, :HEAD], one[:SPAN, :HEAD]], axis=0
            )
            k_ref[pl.ds(late, 2 * SPAN), :] = jnp.concatenate(
                [one[SPAN:, :HEAD], zero[SPAN:, :HEAD]], axis=0
            )
            a, b = zero[:, HEAD:], one[:, HEAD:]
            vt_ref[:HEAD, pl.ds(early, 2 * SPAN)] = jnp.concatenate([a[:, :SPAN], b[:, :SPAN]], axis=1)
            vt_ref[:HEAD, pl.ds(late, 2 * SPAN)] = jnp.concatenate([b[:, SPAN:], a[:, SPAN:]], axis=1)
    k_ref[TOKENS:, :] = jnp.zeros((TILE, HEAD), jnp.bfloat16)
    vt_ref[:HEAD, TOKENS:] = jnp.zeros((HEAD, TILE), jnp.bfloat16)
    vt_ref[HEAD:, :] = jnp.ones((SUMS, TOKENS + TILE), jnp.bfloat16)


def attend_block(scalars, dx, q_ref, k_ref, vt_ref, o_ref, s_scr, m_scr, acc_scr):
    shard = lax.rem(scalars[0] - dx + 4, 4) * 8 + scalars[1] * 2 + scalars[2]
    width = GROUP * SPAN
    key = lax.broadcasted_iota(jnp.int32, (TILE, HEAD), 0)
    token = lax.rem(lax.broadcasted_iota(jnp.int32, (8, HEAD), 1), SPAN)

    def one_half(half, _):
        rows = pl.ds(pl.multiple_of(half * SPAN, SPAN), SPAN)
        block = jnp.where(half == 0, shard, 63 - shard)
        first = block * SPAN
        low = lax.div(doc_start(first, lengths_of(scalars)), HEAD) * HEAD
        count = lax.div(first - low, TILE) + 1
        q_tile = jnp.concatenate(
            [q_ref[rows, h * HEAD : (h + 1) * HEAD] for h in range(GROUP)], axis=0
        )
        q_pos = first + token
        q_start = doc_start(q_pos, lengths_of(scalars))
        m_scr[...] = jnp.full(m_scr.shape, MASKED, jnp.float32)
        acc_scr[...] = jnp.zeros_like(acc_scr)

        def scores(t, tiles):
            top = m_scr[...]
            for u in range(tiles):
                at = pl.multiple_of(low + (t + u) * TILE, HEAD)
                bias = jnp.where(
                    (key <= (q_pos - at)[:1]) & (key >= (q_start - at)[:1]), 0.0, MASKED
                )
                s = lax.dot_general(
                    k_ref[pl.ds(at, TILE), :],
                    q_tile,
                    (((1,), (1,)), ((), ())),
                    preferred_element_type=jnp.float32,
                )
                s = s + jnp.concatenate([bias] * (width // HEAD), axis=1)
                s_scr[t + u] = s
                top = jnp.maximum(top, jnp.max(s.reshape(TILE // 8, 8, width), axis=0))
            m_scr[...] = top

        def weigh(t, tiles):
            weights = []
            for u in range(tiles):
                s = s_scr[t + u].reshape(TILE // 8, 8, width) - m_scr[...][None]
                weights.append(jnp.exp2(s).reshape(TILE, width).astype(jnp.bfloat16))
            at = pl.multiple_of(low + t * TILE, HEAD)
            acc_scr[...] += jnp.dot(
                vt_ref[:, pl.ds(at, tiles * TILE)],
                jnp.concatenate(weights, axis=0),
                preferred_element_type=jnp.float32,
            )

        def in_pairs(step):
            def pair(i, _):
                step(2 * i, 2)
                return 0

            lax.fori_loop(0, lax.div(count, 2), pair, 0)
            pl.when(lax.rem(count, 2) == 1)(lambda: step(count - 1, 1))

        in_pairs(scores)
        m_scr[...] = jnp.broadcast_to(jnp.max(m_scr[...], axis=0, keepdims=True), m_scr.shape)
        in_pairs(weigh)
        out = (acc_scr[:HEAD, :] * (1.0 / acc_scr[HEAD : HEAD + 1, :])).T.astype(jnp.bfloat16)
        for h in range(GROUP):
            o_ref[rows, h * HEAD : (h + 1) * HEAD] = out[h * SPAN : (h + 1) * SPAN]
        return 0

    lax.fori_loop(0, 2, one_half, 0)


def first_kernel(dxs, scalars, *refs):
    n = len(dxs)
    queries, halves, far_ref = refs[:n], refs[n : n + 6], refs[n + 6]
    outs, (k_ref, vt_ref) = refs[n + 7 : 2 * n + 7], refs[2 * n + 7 : 2 * n + 9]
    gather_keys(scalars, halves, far_ref, k_ref, vt_ref)
    for dx, q_ref, o_ref in zip(dxs, queries, outs):
        attend_block(scalars, dx, q_ref, k_ref, vt_ref, o_ref, *refs[2 * n + 9 :])


def next_kernel(dxs, scalars, *refs):
    n = len(dxs)
    queries, (k_ref, vt_ref), outs = refs[:n], refs[n : n + 2], refs[n + 2 : 2 * n + 2]
    for dx, q_ref, o_ref in zip(dxs, queries, outs):
        attend_block(scalars, dx, q_ref, k_ref, vt_ref, o_ref, *refs[2 * n + 2 :])


def first_place_kernel(col_ref, piece_ref, out_ref):
    out_ref[0] = piece_ref[...]


def next_place_kernel(col_ref, piece_ref, old_ref, out_ref):
    out_ref[0] = piece_ref[...]


def place(piece, out, column):
    width = GROUP * HEAD
    first = out is None
    return pl.pallas_call(
        first_place_kernel if first else next_place_kernel,
        out_shape=jax.ShapeDtypeStruct((1, 128, KV_HEADS * width), jnp.bfloat16),
        grid_spec=pltpu.PrefetchScalarGridSpec(
            num_scalar_prefetch=1,
            grid=(1,),
            in_specs=[pl.BlockSpec((128, width), lambda i, col: (0, 0))]
            + ([] if first else [pl.BlockSpec(memory_space=pl.ANY)]),
            out_specs=pl.BlockSpec((1, 128, width), lambda i, col: (0, 0, col[0])),
        ),
        input_output_aliases={} if first else {2: 0},
        compiler_params=room(4),
    )(*((column, held(piece)) if first else (column, held(piece), out)))


def layer(queries, keys, values, doc_lengths, interp_num, interp_den):
    bf16 = jnp.bfloat16
    place_in = jnp.stack([lax.axis_index(a) for a in ("x", "yh", "c")]).astype(jnp.int32)
    scalars = jnp.concatenate([place_in, doc_lengths[0], interp_num, interp_den])
    smem = pl.BlockSpec(memory_space=pltpu.SMEM)
    vmem = pl.BlockSpec(memory_space=pltpu.VMEM)
    piece = pltpu.VMEM((128, GROUP * HEAD), bf16)
    freq = in_hbm(jnp.asarray(frequencies()))
    kv = pl.pallas_call(
        pack_keys_kernel,
        out_shape=pltpu.VMEM((4, 128, 2 * HEAD), bf16),
        in_specs=[smem] * 3 + [vmem] * 3,
        out_specs=vmem,
        name="pack_keys",
        compiler_params=room(12),
    )(in_hbm(doc_lengths), interp_num, interp_den, freq, in_hbm(keys[0]), in_hbm(values[0]))
    packed = pl.pallas_call(
        pack_queries_kernel,
        out_shape=(piece,) * 4,
        in_specs=[smem] + [vmem] * 2,
        out_specs=(vmem,) * 4,
        name="pack_queries",
        compiler_params=room(12),
    )(scalars, freq, queries[0])
    mine = lax.all_to_all(kv, "x", 0, 0, tiled=True)
    swap_cores = functools.partial(lax.ppermute, axis_name="c", perm=[(0, 1), (1, 0)])
    ring = [(y * 2 + c, (y + 1 - 2 * c) % 4 * 2 + c) for y in range(4) for c in range(2)]
    pass_on = functools.partial(lax.ppermute, axis_name=("yh", "c"), perm=ring)
    near_mine = pass_on(mine)
    twin = swap_cores(mine)
    near_twin = pass_on(twin)
    far_mine = pass_on(near_mine)
    other_a = swap_cores(near_mine)
    other_b = swap_cores(near_twin)
    far = lax.all_gather(far_mine, "c", axis=0)
    blocks = (mine, twin, near_mine, near_twin, other_b, other_a, far)
    moved = {0: packed[0]}
    for d in (2, 1, 3):
        moved[d] = lax.ppermute(packed[d], AXES, route(d, 0))
    marked = jnp.minimum(scalars, TOKENS)
    scratch = [
        pltpu.VMEM((ROUNDS, TILE, GROUP * SPAN), jnp.float32),
        pltpu.VMEM((8, GROUP * SPAN), jnp.float32),
        pltpu.VMEM((HEAD + SUMS, GROUP * SPAN), jnp.float32),
    ]
    laid_out = (
        pltpu.VMEM((TOKENS + TILE, HEAD), bf16),
        pltpu.VMEM((HEAD + SUMS, TOKENS + TILE), bf16),
    )
    handed = {}
    ordered = None
    for dxs in CALLS:
        n = len(dxs)
        if ordered is None:
            *results, key_rows, value_columns = pl.pallas_call(
                functools.partial(first_kernel, dxs),
                out_shape=(piece,) * n + laid_out,
                in_specs=[smem] + [vmem] * (n + 7),
                out_specs=(vmem,) * (n + 2),
                scratch_shapes=scratch,
                compiler_params=room(24),
            )(marked, *map(held, [moved[d] for d in dxs]), *map(held, blocks))
            ordered = (key_rows, value_columns)
        else:
            results = pl.pallas_call(
                functools.partial(next_kernel, dxs),
                out_shape=(piece,) * n,
                in_specs=[smem] + [vmem] * (n + 2),
                out_specs=(vmem,) * n,
                scratch_shapes=scratch,
                compiler_params=room(24),
            )(marked, *map(held, [moved[d] for d in dxs]), *map(held, ordered))
        for d, result in zip(dxs, results):
            handed[d] = lax.ppermute(result, AXES, route(-d, 1))
    out = None
    for d in sum(CALLS, ()):
        out = place(handed[d], out, (marked[:1] + d) % 4)
    return out


def solution(mesh):
    fine = Mesh(mesh.devices.reshape(SIZES), AXES)
    ctx, section = ("x", "yh", "c"), ("yl", "z")
    placed = (
        P(section, ctx, None),
        P(section, ctx, None),
        P(section, ctx, None),
        P(section, None),
        P(),
        P(),
    )
    return jax.shard_map(
        layer, mesh=fine, in_specs=placed, out_specs=P(section, ctx, None), check_vma=False
    )
```
